32 devices in a mesh: groups: 2 (over y), space: 4 (over x, core), chan: 4 (over z).
Axes of the slice: x: 2, y: 2, z: 4, core: 2. Of those that a mesh axis runs over, the one named last changes fastest.
Arguments:
- fields: bfloat16 [1024, 16, 256], P('chan', ('groups', 'space')), parts along dimension 1, may hold values from -6 to 6
- conv_weight: bfloat16 [27, 1024, 1024], P(None, 'chan', 'space'), may hold values from -0.0390625 to 0.0390625
Outputs:
- convolved: bfloat16 [1024, 16, 256], P('chan', ('groups', 'space')), parts along dimension 1
The draws below stay inside these ranges and needn't reach their ends.
There are 2 independent parts, one for each index of `groups`. The reference program is written for one: setup_inputs(seed, part) draws one part's arguments, and reference() takes and returns one part's arrays. A program takes and returns all parts, laid end to end along the dimension named above; an argument that names none is the same for every part. Nothing has to cross between parts.
All inputs are finite; a program needn't handle non-finite values.
Results may differ from the reference program's by a relative error of at most 0.001.
Values may be sent and summed in bfloat16 or wider, within the bound.
A program may use at most 128 MiB of HBM per device.

```python
import jax
import jax.numpy as jnp
from jax import lax

C = 1024
NY = 16
NZ = 16
NX = 8


def block_levels(own_key, dims, cuts, low, top_value):
    loudness, own = 1.0, jax.random.fold_in(own_key, 6)
    for dim, blocks in cuts:
        heights = jnp.exp(jax.random.uniform(jax.random.fold_in(own, dim), (blocks,), jnp.float32, low / len(cuts), top_value / len(cuts)))
        loudness = loudness * jnp.repeat(heights, dims[dim] // blocks).reshape([-1 if axis == dim else 1 for axis in range(len(dims))])
    return loudness


def noise(rng, extent, spread, reach, cuts=(), held_as=jnp.bfloat16):
    values = jax.random.normal(rng, extent, jnp.float32) * spread
    if len(cuts) > 0:
        values = block_levels(rng, extent, cuts, -0.22, 0.18) * values
    return jnp.clip(values, min=-reach, max=reach).astype(held_as)


def setup_inputs(seed: int = 0, part: int = 0) -> dict:
    arg_keys = jax.random.split(jax.random.key(seed), 3)
    own_keys = jax.random.split(jax.random.fold_in(arg_keys[2], part), 3)
    return {
        "fields": noise(own_keys[0], (C, NX, NY * NZ), 1.0, 6.0, ((0, 4), (1, 4))),
        "conv_weight": noise(arg_keys[1], (27, C, C), (27 * C) ** -0.5, 0.0390625, ((1, 4), (2, 4))),
    }


def reference(fields, conv_weight):
    depth = fields.shape[1]
    source = fields.astype(jnp.float32).reshape(C, depth, NY, NZ)
    padded = jnp.pad(source, ((0, 0), (1, 1), (1, 1), (1, 1)))
    summed = jnp.zeros((C, depth * NY * NZ), jnp.float32)
    for step_x in range(3):
        for step_y in range(3):
            for step_z in range(3):
                matrix = conv_weight[9 * step_x + 3 * step_y + step_z].astype(jnp.float32)
                window = padded[:, step_x:step_x + depth, step_y:step_y + NY, step_z:step_z + NZ].reshape(C, depth * NY * NZ)
                summed = summed + jnp.dot(matrix, window, precision=lax.Precision.HIGHEST, preferred_element_type=jnp.float32)
    return summed.reshape(C, depth, NY * NZ).astype(jnp.bfloat16)
```

```python
import functools

import jax
import jax.numpy as jnp
from jax import lax
from jax.experimental import pallas as pl
from jax.experimental.pallas import tpu as pltpu
from jax.sharding import PartitionSpec as P

NZ = 16
TAPS = 27
MESH = pl.DeviceIdType.MESH


def kernel(
    S, n, r, x_ref, w_ref, out_ref,
    xz, xr, xs, wv, psend, precv, xsend, xrecv, own,
    w_sem, up_sem, down_sem, z_sem, a_send, a_recv, p_send, p_recv, q_send, q_recv,
):
    depth, cells, chb = x_ref.shape
    I = r * chb
    nx = S // 2
    planes = S * depth
    s = lax.axis_index("space")
    z = lax.axis_index("chan")
    x = s // 2
    k = s % 2
    partner = x * 2 + (1 - k)

    for t in range(TAPS):
        pltpu.make_async_copy(w_ref.at[t], wv.at[:, t * I : (t + 1) * I], w_sem.at[t]).start()

    barrier = pltpu.get_barrier_semaphore()

    @pl.when(z > 0)
    def _():
        pl.semaphore_signal(barrier, inc=1, device_id={"chan": z - 1}, device_id_type=MESH)

    @pl.when(z < n - 1)
    def _():
        pl.semaphore_signal(barrier, inc=1, device_id={"chan": z + 1}, device_id_type=MESH)

    for so in range(1, S):
        pl.semaphore_signal(
            barrier, inc=1, device_id={"space": lax.rem(s + so, S)}, device_id_type=MESH
        )
    here = jnp.where(z > 0, 1, 0) + jnp.where(z < n - 1, 1, 0) + (S - 1)
    pl.semaphore_wait(barrier, here)

    def hop(src, b, p, sem, to):
        return pltpu.make_async_remote_copy(
            src_ref=src, dst_ref=xz.at[b, p], send_sem=sem, recv_sem=z_sem.at[b, p],
            device_id={"chan": to}, device_id_type=MESH,
        )

    def across(src, b, p):
        return pltpu.make_async_remote_copy(
            src_ref=src, dst_ref=xr.at[s, b % r, p], send_sem=a_send.at[b, p],
            recv_sem=a_recv.at[s, b % r, p],
            device_id={"space": b // r}, device_id_type=MESH,
        )

    def source(h, b, p):
        return x_ref.at[p] if h == 0 else xz.at[b, p]

    def up(h, p):
        return hop(source(h, z - h, p), z - h, p, up_sem.at[h, p], z + 1)

    def down(h, p):
        return hop(source(h, z + h, p), z + h, p, down_sem.at[h, p], z - 1)

    for h in range(n):
        for p in range(depth):
            if h > 0:
                @pl.when(z - h >= 0)
                def _():
                    hop(xz.at[z - h, p], z - h, p, up_sem.at[0, p], z).wait_recv()

            if h < n - 1:
                @pl.when((z - h >= 0) & (z < n - 1))
                def _():
                    up(h, p).start()

            if h > 0:
                @pl.when(z + h < n)
                def _():
                    hop(xz.at[z + h, p], z + h, p, up_sem.at[0, p], z).wait_recv()

            if h < n - 1:
                @pl.when((z + h < n) & (z > 0))
                def _():
                    down(h, p).start()

            for sign in (-1, 1) if h > 0 else (1,):
                b = z + sign * h

                @pl.when((b >= 0) & (b < n) & (b // r != s))
                def _():
                    across(source(h, b, p), b, p).start()

    rows = lax.broadcasted_iota(jnp.int32, (cells, chb), 0) % NZ
    zero_row = jnp.zeros((NZ, I), xs.dtype)
    zero_plane = jnp.zeros(xs.shape[2:], xs.dtype)
    for c in range(3):
        xs[0, c] = zero_plane
        xs[planes + 1, c] = zero_plane

        @pl.loop(1, planes + 1)
        def _(q):
            xs[q, c, :NZ, :] = zero_row
            xs[q, c, NZ + cells :, :] = zero_row

    def prepare(v, q, j):
        wide = v.astype(jnp.float32)
        before = jnp.where(rows == 0, 0.0, pltpu.roll(wide, 1, 0))
        after = jnp.where(rows == NZ - 1, 0.0, pltpu.roll(wide, cells - 1, 0))
        lanes = slice(j * chb, (j + 1) * chb)
        xs[q + 1, 0, NZ : NZ + cells, lanes] = before.astype(xs.dtype)
        xs[q + 1, 1, NZ : NZ + cells, lanes] = v
        xs[q + 1, 2, NZ : NZ + cells, lanes] = after.astype(xs.dtype)

    for j in range(r):
        @pl.when(z == s * r + j)
        def _():
            @pl.loop(0, depth)
            def _(p):
                prepare(x_ref[p], s * depth + p, j)

        @pl.when(z != s * r + j)
        def _():
            @pl.loop(0, depth)
            def _(p):
                prepare(xz[s * r + j, p], s * depth + p, j)

    @pl.loop(1, S)
    def _(so):
        src = lax.rem(s + so, S)

        @pl.loop(0, depth)
        def _(p):
            for j in range(r):
                pltpu.make_async_remote_copy(
                    src_ref=xr.at[src, j, p], dst_ref=xr.at[src, j, p],
                    send_sem=a_send.at[0, p], recv_sem=a_recv.at[src, j, p],
                    device_id={"space": src}, device_id_type=MESH,
                ).wait_recv()
                prepare(xr[src, j, p], src * depth + p, j)

    for t in range(TAPS):
        pltpu.make_async_copy(w_ref.at[t], wv.at[:, t * I : (t + 1) * I], w_sem.at[t]).wait()

    def partial(q):
        window = jnp.concatenate(
            [
                xs[q + a, c, NZ * b : NZ * b + cells, :]
                for a in range(3)
                for b in range(3)
                for c in range(3)
            ],
            axis=1,
        )
        return lax.dot_general(
            window, wv[...], (((1,), (1,)), ((), ())), preferred_element_type=jnp.float32
        )

    def to_partner(m):
        return pltpu.make_async_remote_copy(
            src_ref=psend.at[m], dst_ref=precv.at[m], send_sem=p_send.at[m],
            recv_sem=p_recv.at[m], device_id={"space": partner}, device_id_type=MESH,
        )

    def to_chip(m, there):
        return pltpu.make_async_remote_copy(
            src_ref=xsend.at[m], dst_ref=xrecv.at[m], send_sem=q_send.at[m],
            recv_sem=q_recv.at[m], device_id={"space": there}, device_id_type=MESH,
        )

    @pl.loop(0, 2 * planes // 2)
    def _(i):
        m = i // 2
        mine = i % 2
        hops = m // depth + 1
        p = m % depth
        far = lax.rem(x + hops, nx)
        core = jnp.where(mine == 1, k, 1 - k)
        total = partial((far * 2 + core) * depth + p)

        @pl.when(mine == 0)
        def _():
            psend[m] = total
            to_partner(m).start()

        @pl.when(mine == 1)
        def _():
            to_partner(m).wait_recv()

            @pl.when(hops < nx)
            def _():
                xsend[m] = total + precv[m]
                to_chip(m, far * 2 + k).start()

            @pl.when(hops == nx)
            def _():
                own[p] = total + precv[m]

    for p in range(depth):
        total = own[p]
        for hops in range(1, nx):
            m = (hops - 1) * depth + p
            to_chip(m, partner).wait_recv()
            total = total + xrecv[m]
        out_ref[p] = total.astype(out_ref.dtype)

    for h in range(n):
        for p in range(depth):
            if h < n - 1:
                @pl.when((z - h >= 0) & (z < n - 1))
                def _():
                    up(h, p).wait_send()

                @pl.when((z + h < n) & (z > 0))
                def _():
                    down(h, p).wait_send()

            for sign in (-1, 1) if h > 0 else (1,):
                b = z + sign * h

                @pl.when((b >= 0) & (b < n) & (b // r != s))
                def _():
                    across(source(h, b, p), b, p).wait_send()

    for m in range(nx * depth):
        to_partner(m).wait_send()
        if m < (nx - 1) * depth:
            to_chip(m, partner).wait_send()


def local(S, n, fields, conv_weight):
    chb, depth, cells = fields.shape
    owned, I = conv_weight.shape[1:]
    r = I // chb
    nx = S // 2
    planes = S * depth
    bf16, f32 = jnp.bfloat16, jnp.float32
    dma = pltpu.SemaphoreType.DMA
    x = jnp.transpose(fields, (1, 2, 0))
    result = pl.pallas_call(
        functools.partial(kernel, S, n, r),
        out_shape=jax.ShapeDtypeStruct((depth, cells, owned), bf16),
        in_specs=[
            pl.BlockSpec(memory_space=pltpu.VMEM),
            pl.BlockSpec(memory_space=pl.ANY),
        ],
        out_specs=pl.BlockSpec(memory_space=pltpu.VMEM),
        scratch_shapes=[
            pltpu.VMEM((n, depth, cells, chb), bf16),
            pltpu.VMEM((S, r, depth, cells, chb), bf16),
            pltpu.VMEM((planes + 2, 3, cells + 2 * NZ, I), bf16),
            pltpu.VMEM((owned, TAPS * I), bf16),
            pltpu.VMEM((nx * depth, cells, owned), f32),
            pltpu.VMEM((nx * depth, cells, owned), f32),
            pltpu.VMEM(((nx - 1) * depth, cells, owned), f32),
            pltpu.VMEM(((nx - 1) * depth, cells, owned), f32),
            pltpu.VMEM((depth, cells, owned), f32),
            dma((TAPS,)),
            dma((n, depth)),
            dma((n, depth)),
            dma((n, depth)),
            dma((n, depth)),
            dma((S, r, depth)),
            dma((nx * depth,)),
            dma((nx * depth,)),
            dma((nx * depth,)),
            dma((nx * depth,)),
        ],
        compiler_params=pltpu.CompilerParams(
            collective_id=0, has_side_effects=True, vmem_limit_bytes=50 * 1024 * 1024
        ),
    )(x, conv_weight)
    return jnp.transpose(result, (2, 0, 1))


def solution(mesh):
    return jax.shard_map(
        functools.partial(local, mesh.shape["space"], mesh.shape["chan"]),
        mesh=mesh,
        in_specs=(P("chan", ("groups", "space"), None), P(None, "chan", "space")),
        out_specs=P("chan", ("groups", "space"), None),
        check_vma=False,
    )
```

```python
import functools

import jax
import jax.numpy as jnp
from jax import lax
from jax.experimental import pallas as pl
from jax.experimental.pallas import tpu as pltpu
from jax.sharding import PartitionSpec as P

NZ = 16
TAPS = 27
MESH = pl.DeviceIdType.MESH


def kernel(
    S, n, r, x_ref, w_ref, out_ref,
    xz, xr, xs, wv, psend, precv, xsend, xrecv, own, early,
    w_sem, up_sem, down_sem, z_sem, a_send, a_recv, p_send, p_recv, q_send, q_recv,
):
    depth, cells, chb = x_ref.shape
    I = r * chb
    nx = S // 2
    planes = S * depth
    s = lax.axis_index("space")
    z = lax.axis_index("chan")
    x = s // 2
    k = s % 2
    partner = x * 2 + (1 - k)

    for t in range(TAPS):
        pltpu.make_async_copy(w_ref.at[t], wv.at[:, t * I : (t + 1) * I], w_sem.at[t]).start()

    barrier = pltpu.get_barrier_semaphore()

    for so in range(S):
        for step, there in ((-1, z > 0), (1, z < n - 1)):
            @pl.when(there)
            def _():
                pl.semaphore_signal(
                    barrier, inc=1, device_id={"space": lax.rem(s + so, S), "chan": z + step},
                    device_id_type=MESH,
                )

    for so in range(1, S):
        pl.semaphore_signal(
            barrier, inc=1, device_id={"space": lax.rem(s + so, S)}, device_id_type=MESH
        )
    here = jnp.where(z > 0, S, 0) + jnp.where(z < n - 1, S, 0) + (S - 1)
    pl.semaphore_wait(barrier, here)

    def hop(src, b, p, sem, to):
        return pltpu.make_async_remote_copy(
            src_ref=src, dst_ref=xz.at[b, p], send_sem=sem, recv_sem=z_sem.at[b, p],
            device_id={"chan": to}, device_id_type=MESH,
        )

    def across(src, b, p):
        return pltpu.make_async_remote_copy(
            src_ref=src, dst_ref=xr.at[s, b % r, p], send_sem=a_send.at[b, p],
            recv_sem=a_recv.at[s, b % r, p],
            device_id={"space": b // r}, device_id_type=MESH,
        )

    def source(h, b, p):
        return x_ref.at[p] if h == 0 else xz.at[b, p]

    def up(h, p):
        return hop(source(h, z - h, p), z - h, p, up_sem.at[h, p], z + 1)

    def down(h, p):
        return hop(source(h, z + h, p), z + h, p, down_sem.at[h, p], z - 1)

    def slanted(h, b, p, sem, to):
        return pltpu.make_async_remote_copy(
            src_ref=source(h, b, p), dst_ref=xr.at[s, b % r, p], send_sem=sem,
            recv_sem=a_recv.at[s, b % r, p],
            device_id={"space": b // r, "chan": to}, device_id_type=MESH,
        )

    def direct(h, b, to, end):
        return (to == end) & (b // r != s)

    def forward(h, p):
        for b, sign, end, send in ((z - h, 1, n - 1, up), (z + h, -1, 0, down)):
            valid = (b >= 0) & (b < n)
            relay = valid
            if h > 0:
                relay = valid & ~direct(h - 1, b, z, end)

                @pl.when(relay)
                def _():
                    hop(xz.at[b, p], b, p, up_sem.at[0, p], z).wait_recv()

            if h < n - 1:
                straight = direct(h, b, z + sign, end)

                @pl.when(valid & (z != end) & ~straight)
                def _():
                    send(h, p).start()

                @pl.when(valid & (z != end) & straight)
                def _():
                    sem = (up_sem if sign == 1 else down_sem).at[h, p]
                    slanted(h, b, p, sem, z + sign).start()

            if h > 0 or sign == 1:
                @pl.when(relay & (b // r != s))
                def _():
                    across(source(h, b, p), b, p).start()

    for p in range(depth):
        forward(0, p)

    rows = lax.broadcasted_iota(jnp.int32, (cells, chb), 0) % NZ
    zero_row = jnp.zeros((NZ, I), xs.dtype)
    zero_plane = jnp.zeros(xs.shape[2:], xs.dtype)
    for c in range(3):
        xs[0, c] = zero_plane
        xs[planes + 1, c] = zero_plane

        @pl.loop(1, planes + 1)
        def _(q):
            xs[q, c, :NZ, :] = zero_row
            xs[q, c, NZ + cells :, :] = zero_row

    def prepare(v, q, j):
        wide = v.astype(jnp.float32)
        before = jnp.where(rows == 0, 0.0, pltpu.roll(wide, 1, 0))
        after = jnp.where(rows == NZ - 1, 0.0, pltpu.roll(wide, cells - 1, 0))
        lanes = slice(j * chb, (j + 1) * chb)
        xs[q + 1, 0, NZ : NZ + cells, lanes] = before.astype(xs.dtype)
        xs[q + 1, 1, NZ : NZ + cells, lanes] = v
        xs[q + 1, 2, NZ : NZ + cells, lanes] = after.astype(xs.dtype)

    for h in range(1, n - 1):
        for p in range(depth):
            forward(h, p)

    def fetch_own(p):
        for j in range(r):
            @pl.when(z == s * r + j)
            def _():
                prepare(x_ref[p], s * depth + p, j)

            @pl.when(z != s * r + j)
            def _():
                prepare(xz[s * r + j, p], s * depth + p, j)

    def fetch(src, p):
        for j in range(r):
            pltpu.make_async_remote_copy(
                src_ref=xr.at[src, j, p], dst_ref=xr.at[src, j, p],
                send_sem=a_send.at[0, p], recv_sem=a_recv.at[src, j, p],
                device_id={"space": src}, device_id_type=MESH,
            ).wait_recv()
            prepare(xr[src, j, p], src * depth + p, j)

    def fetch_far(p):
        @pl.loop(0, S)
        def _(src):
            @pl.when(src // 2 != x)
            def _():
                fetch(src, p)

    for t in range(TAPS):
        pltpu.make_async_copy(w_ref.at[t], wv.at[:, t * I : (t + 1) * I], w_sem.at[t]).wait()

    def terms(q, taps):
        window = jnp.concatenate(
            [
                xs[q + a, c, NZ * b : NZ * b + cells, :]
                for a in taps
                for b in range(3)
                for c in range(3)
            ],
            axis=1,
        )
        if len(taps) == 3:
            held = wv[...]
        else:
            held = jnp.concatenate([wv[:, 9 * I * a : 9 * I * (a + 1)] for a in taps], axis=1)
        return lax.dot_general(
            window, held, (((1,), (1,)), ((), ())), preferred_element_type=jnp.float32
        )

    def parity(p):
        return tuple(a for a in range(3) if (p + a - 1) % 2 == 0)

    def target(hops, mine):
        far = lax.rem(x + hops, nx)
        return far * 2 + jnp.where(mine == 1, k, 1 - k)

    def start_early():
        fetch_own(0)
        fetch(partner, 0)
        fetch_far(0)

        @pl.loop(0, 2 * (nx - 1))
        def _(i):
            dest = target(i // 2 + 1, i % 2)
            for p in range(depth):
                early[i, p] = terms(dest * depth + p, parity(p))

    last = jnp.abs(z - s // r) if r == 1 else n - 1

    @pl.when(last < n - 1)
    def _():
        start_early()

    forward(n - 1, 0)

    @pl.when(last == n - 1)
    def _():
        start_early()

    for p in range(1, depth):
        forward(n - 1, p)

    for p in range(1, depth):
        fetch_own(p)
        fetch(partner, p)
        fetch_far(p)

    def to_partner(m):
        return pltpu.make_async_remote_copy(
            src_ref=psend.at[m], dst_ref=precv.at[m], send_sem=p_send.at[m],
            recv_sem=p_recv.at[m], device_id={"space": partner}, device_id_type=MESH,
        )

    def to_chip(m, there):
        return pltpu.make_async_remote_copy(
            src_ref=xsend.at[m], dst_ref=xrecv.at[m], send_sem=q_send.at[m],
            recv_sem=q_recv.at[m], device_id={"space": there}, device_id_type=MESH,
        )

    def finish(m, p, hops, mine, total):
        @pl.when(mine == 0)
        def _():
            psend[m] = total
            to_partner(m).start()

        @pl.when(mine == 1)
        def _():
            to_partner(m).wait_recv()

            @pl.when(hops < nx)
            def _():
                xsend[m] = total + precv[m]
                to_chip(m, target(hops, 1)).start()

            @pl.when(hops == nx)
            def _():
                own[p] = total + precv[m]

    for p in range(depth - 1, -1, -1):
        rest = tuple(a for a in range(3) if a not in parity(p))
        @pl.loop(0, 2 * (nx - 1))
        def _(i):
            hops = i // 2 + 1
            mine = i % 2
            total = early[i, p] + terms(target(hops, mine) * depth + p, rest)
            finish((hops - 1) * depth + p, p, hops, mine, total)

    @pl.loop(0, 2 * depth)
    def _(i):
        p = i // 2
        mine = i % 2
        total = terms(target(nx, mine) * depth + p, (0, 1, 2))
        finish((nx - 1) * depth + p, p, nx, mine, total)

    for p in range(depth):
        total = own[p]
        for hops in range(1, nx):
            m = (hops - 1) * depth + p
            to_chip(m, partner).wait_recv()
            total = total + xrecv[m]
        out_ref[p] = total.astype(out_ref.dtype)

    for h in range(n):
        for p in range(depth):
            if h < n - 1:
                @pl.when((z - h >= 0) & (z < n - 1))
                def _():
                    up(h, p).wait_send()

                @pl.when((z + h < n) & (z > 0))
                def _():
                    down(h, p).wait_send()

            for b, sign, end in ((z - h, 1, n - 1), (z + h, -1, 0)):
                relay = (b >= 0) & (b < n) & (b // r != s)
                if h > 0:
                    relay = relay & ~direct(h - 1, b, z, end)

                if h > 0 or sign == 1:
                    @pl.when(relay)
                    def _():
                        across(source(h, b, p), b, p).wait_send()

    for m in range(nx * depth):
        to_partner(m).wait_send()
        if m < (nx - 1) * depth:
            to_chip(m, partner).wait_send()


def local(S, n, fields, conv_weight):
    chb, depth, cells = fields.shape
    owned, I = conv_weight.shape[1:]
    r = I // chb
    nx = S // 2
    planes = S * depth
    bf16, f32 = jnp.bfloat16, jnp.float32
    dma = pltpu.SemaphoreType.DMA
    x = jnp.transpose(fields, (1, 2, 0))
    result = pl.pallas_call(
        functools.partial(kernel, S, n, r),
        out_shape=jax.ShapeDtypeStruct((depth, cells, owned), bf16),
        in_specs=[
            pl.BlockSpec(memory_space=pltpu.VMEM),
            pl.BlockSpec(memory_space=pl.ANY),
        ],
        out_specs=pl.BlockSpec(memory_space=pltpu.VMEM),
        scratch_shapes=[
            pltpu.VMEM((n, depth, cells, chb), bf16),
            pltpu.VMEM((S, r, depth, cells, chb), bf16),
            pltpu.VMEM((planes + 2, 3, cells + 2 * NZ, I), bf16),
            pltpu.VMEM((owned, TAPS * I), bf16),
            pltpu.VMEM((nx * depth, cells, owned), f32),
            pltpu.VMEM((nx * depth, cells, owned), f32),
            pltpu.VMEM(((nx - 1) * depth, cells, owned), f32),
            pltpu.VMEM(((nx - 1) * depth, cells, owned), f32),
            pltpu.VMEM((depth, cells, owned), f32),
            pltpu.VMEM((2 * (nx - 1), depth, cells, owned), f32),
            dma((TAPS,)),
            dma((n, depth)),
            dma((n, depth)),
            dma((n, depth)),
            dma((n, depth)),
            dma((S, r, depth)),
            dma((nx * depth,)),
            dma((nx * depth,)),
            dma((nx * depth,)),
            dma((nx * depth,)),
        ],
        compiler_params=pltpu.CompilerParams(
            collective_id=0, has_side_effects=True, vmem_limit_bytes=62 * 1024 * 1024
        ),
    )(x, conv_weight)
    return jnp.transpose(result, (2, 0, 1))


def solution(mesh):
    return jax.shard_map(
        functools.partial(local, mesh.shape["space"], mesh.shape["chan"]),
        mesh=mesh,
        in_specs=(P("chan", ("groups", "space"), None), P(None, "chan", "space")),
        out_specs=P("chan", ("groups", "space"), None),
        check_vma=False,
    )
```

```python
import functools

import jax
import jax.numpy as jnp
from jax import lax
from jax.experimental import pallas as pl
from jax.experimental.pallas import tpu as pltpu
from jax.sharding import PartitionSpec as P

NZ = 16
TAPS = 27
MESH = pl.DeviceIdType.MESH


def kernel(
    S, n, r, x_ref, w_ref, out_ref,
    xz, xr, xs, wv, psend, precv, xsend, xrecv, own,
    w_sem, up_sem, down_sem, z_sem, a_send, a_recv, p_send, p_recv, q_send, q_recv,
):
    depth, cells, chb = x_ref.shape
    I = r * chb
    nx = S // 2
    planes = S * depth
    s = lax.axis_index("space")
    z = lax.axis_index("chan")
    x = s // 2
    k = s % 2
    partner = x * 2 + (1 - k)

    for t in range(TAPS):
        pltpu.make_async_copy(w_ref.at[t], wv.at[:, t * I : (t + 1) * I], w_sem.at[t]).start()

    barrier = pltpu.get_barrier_semaphore()

    for so in range(S):
        for step, there in ((-1, z > 0), (1, z < n - 1)):
            @pl.when(there)
            def _():
                pl.semaphore_signal(
                    barrier, inc=1, device_id={"space": lax.rem(s + so, S), "chan": z + step},
                    device_id_type=MESH,
                )

    for so in range(1, S):
        pl.semaphore_signal(
            barrier, inc=1, device_id={"space": lax.rem(s + so, S)}, device_id_type=MESH
        )
    here = jnp.where(z > 0, S, 0) + jnp.where(z < n - 1, S, 0) + (S - 1)
    pl.semaphore_wait(barrier, here)

    split = cells // 2 + NZ
    spans = ((0, split), (split, cells - split))
    rows_out = cells // 2

    def part(ref, u):
        return ref.at[u % depth, pl.ds(*spans[u // depth])]

    def hop(src, b, p, sem, to):
        return pltpu.make_async_remote_copy(
            src_ref=src, dst_ref=part(xz.at[b], p), send_sem=sem, recv_sem=z_sem.at[b, p],
            device_id={"chan": to}, device_id_type=MESH,
        )

    def across(src, b, p):
        return pltpu.make_async_remote_copy(
            src_ref=src, dst_ref=part(xr.at[s, b % r], p), send_sem=a_send.at[b, p],
            recv_sem=a_recv.at[s, b % r, p],
            device_id={"space": b // r}, device_id_type=MESH,
        )

    def source(h, b, p):
        return part(x_ref, p) if h == 0 else part(xz.at[b], p)

    def up(h, p):
        return hop(source(h, z - h, p), z - h, p, up_sem.at[h, p], z + 1)

    def down(h, p):
        return hop(source(h, z + h, p), z + h, p, down_sem.at[h, p], z - 1)

    def slanted(h, b, p, sem, to):
        return pltpu.make_async_remote_copy(
            src_ref=source(h, b, p), dst_ref=part(xr.at[s, b % r], p), send_sem=sem,
            recv_sem=a_recv.at[s, b % r, p],
            device_id={"space": b // r, "chan": to}, device_id_type=MESH,
        )

    def direct(h, b, to, end):
        return (to == end) & (b // r != s)

    def forward(h, p):
        for b, sign, end, send in ((z - h, 1, n - 1, up), (z + h, -1, 0, down)):
            valid = (b >= 0) & (b < n)
            relay = valid
            if h > 0:
                relay = valid & ~direct(h - 1, b, z, end)

                @pl.when(relay)
                def _():
                    hop(part(xz.at[b], p), b, p, up_sem.at[0, p], z).wait_recv()

            if h < n - 1:
                straight = direct(h, b, z + sign, end)

                @pl.when(valid & (z != end) & ~straight)
                def _():
                    send(h, p).start()

                @pl.when(valid & (z != end) & straight)
                def _():
                    sem = (up_sem if sign == 1 else down_sem).at[h, p]
                    slanted(h, b, p, sem, z + sign).start()

            if h > 0 or sign == 1:
                @pl.when(relay & (b // r != s))
                def _():
                    across(source(h, b, p), b, p).start()

    for p in range(2 * depth):
        forward(0, p)

    zero_row = jnp.zeros((NZ, I), xs.dtype)
    zero_plane = jnp.zeros(xs.shape[2:], xs.dtype)
    for c in range(3):
        xs[0, c] = zero_plane
        xs[planes + 1, c] = zero_plane

        @pl.loop(1, planes + 1)
        def _(q):
            xs[q, c, :NZ, :] = zero_row
            xs[q, c, NZ + cells :, :] = zero_row

    def prepare(ref, u, q, j):
        v = part(ref, u)[...]
        start, size = spans[u // depth]
        rows = lax.broadcasted_iota(jnp.int32, (size, chb), 0) % NZ
        wide = v.astype(jnp.float32)
        before = jnp.where(rows == 0, 0.0, pltpu.roll(wide, 1, 0))
        after = jnp.where(rows == NZ - 1, 0.0, pltpu.roll(wide, size - 1, 0))
        lanes = slice(j * chb, (j + 1) * chb)
        to = slice(NZ + start, NZ + start + size)
        xs[q + 1, 0, to, lanes] = before.astype(xs.dtype)
        xs[q + 1, 1, to, lanes] = v
        xs[q + 1, 2, to, lanes] = after.astype(xs.dtype)

    for h in range(1, n - 1):
        for p in range(2 * depth):
            forward(h, p)

    def fetch_half(half):
        for p in range(depth):
            u = half * depth + p
            for j in range(r):
                @pl.when(z == s * r + j)
                def _():
                    prepare(x_ref, u, s * depth + p, j)

                @pl.when(z != s * r + j)
                def _():
                    prepare(xz.at[s * r + j], u, s * depth + p, j)

            @pl.loop(1, S)
            def _(so):
                src = lax.rem(s + so, S)
                for j in range(r):
                    view = part(xr.at[src, j], u)
                    pltpu.make_async_remote_copy(
                        src_ref=view, dst_ref=view,
                        send_sem=a_send.at[0, u], recv_sem=a_recv.at[src, j, u],
                        device_id={"space": src}, device_id_type=MESH,
                    ).wait_recv()
                    prepare(xr.at[src, j], u, src * depth + p, j)

    for t in range(TAPS):
        pltpu.make_async_copy(w_ref.at[t], wv.at[:, t * I : (t + 1) * I], w_sem.at[t]).wait()

    def partial(dest, half):
        window = jnp.concatenate(
            [
                jnp.concatenate(
                    [
                        xs[
                            dest * depth + p + a, c,
                            NZ * b + half * rows_out : NZ * b + (half + 1) * rows_out, :,
                        ]
                        for p in range(depth)
                    ],
                    axis=0,
                )
                for a in range(3)
                for b in range(3)
                for c in range(3)
            ],
            axis=1,
        )
        return lax.dot_general(
            window, wv[...], (((1,), (1,)), ((), ())), preferred_element_type=jnp.float32
        )

    def target(hops, mine):
        far = lax.rem(x + hops, nx)
        return far * 2 + jnp.where(mine == 1, k, 1 - k)

    def half_of(ref, m, half):
        return ref.at[m, half]

    def to_partner(m, half):
        return pltpu.make_async_remote_copy(
            src_ref=half_of(psend, m, half), dst_ref=half_of(precv, m, half),
            send_sem=p_send.at[m, half], recv_sem=p_recv.at[m, half],
            device_id={"space": partner}, device_id_type=MESH,
        )

    def to_chip(m, half, there):
        return pltpu.make_async_remote_copy(
            src_ref=half_of(xsend, m, half), dst_ref=half_of(xrecv, m, half),
            send_sem=q_send.at[m, half], recv_sem=q_recv.at[m, half],
            device_id={"space": there}, device_id_type=MESH,
        )

    def reduce_half(half, first, stop):
        @pl.loop(2 * first, 2 * stop)
        def _(i):
            m = i // 2
            mine = i % 2
            total = partial(target(m + 1, mine), half)

            @pl.when(mine == 0)
            def _():
                psend[m, half] = total
                to_partner(m, half).start()

            @pl.when(mine == 1)
            def _():
                to_partner(m, half).wait_recv()
                if first < nx - 1:
                    xsend[m, half] = total + precv[m, half]
                    to_chip(m, half, target(m + 1, 1)).start()
                else:
                    own[half] = total + precv[m, half]

    for p in range(depth):
        forward(n - 1, p)
    fetch_half(0)
    reduce_half(0, 0, nx - 1)
    for p in range(depth, 2 * depth):
        forward(n - 1, p)
    fetch_half(1)
    reduce_half(1, 0, nx - 1)
    for half in range(2):
        reduce_half(half, nx - 1, nx)

    for half in range(2):
        total = own[half]
        for m in range(nx - 1):
            to_chip(m, half, partner).wait_recv()
            total = total + xrecv[m, half]
        for p in range(depth):
            out_ref[p, half * rows_out : (half + 1) * rows_out, :] = total[
                p * rows_out : (p + 1) * rows_out
            ].astype(out_ref.dtype)

    for h in range(n):
        for p in range(2 * depth):
            if h < n - 1:
                @pl.when((z - h >= 0) & (z < n - 1))
                def _():
                    up(h, p).wait_send()

                @pl.when((z + h < n) & (z > 0))
                def _():
                    down(h, p).wait_send()

            for b, sign, end in ((z - h, 1, n - 1), (z + h, -1, 0)):
                relay = (b >= 0) & (b < n) & (b // r != s)
                if h > 0:
                    relay = relay & ~direct(h - 1, b, z, end)

                if h > 0 or sign == 1:
                    @pl.when(relay)
                    def _():
                        across(source(h, b, p), b, p).wait_send()

    for m in range(nx):
        for half in range(2):
            to_partner(m, half).wait_send()
            if m < nx - 1:
                to_chip(m, half, partner).wait_send()


def local(S, n, fields, conv_weight):
    chb, depth, cells = fields.shape
    owned, I = conv_weight.shape[1:]
    r = I // chb
    nx = S // 2
    planes = S * depth
    bf16, f32 = jnp.bfloat16, jnp.float32
    dma = pltpu.SemaphoreType.DMA
    x = jnp.transpose(fields, (1, 2, 0))
    result = pl.pallas_call(
        functools.partial(kernel, S, n, r),
        out_shape=jax.ShapeDtypeStruct((depth, cells, owned), bf16),
        in_specs=[
            pl.BlockSpec(memory_space=pltpu.VMEM),
            pl.BlockSpec(memory_space=pl.ANY),
        ],
        out_specs=pl.BlockSpec(memory_space=pltpu.VMEM),
        scratch_shapes=[
            pltpu.VMEM((n, depth, cells, chb), bf16),
            pltpu.VMEM((S, r, depth, cells, chb), bf16),
            pltpu.VMEM((planes + 2, 3, cells + 2 * NZ, I), bf16),
            pltpu.VMEM((owned, TAPS * I), bf16),
            pltpu.VMEM((nx, 2, depth * cells // 2, owned), f32),
            pltpu.VMEM((nx, 2, depth * cells // 2, owned), f32),
            pltpu.VMEM((nx - 1, 2, depth * cells // 2, owned), f32),
            pltpu.VMEM((nx - 1, 2, depth * cells // 2, owned), f32),
            pltpu.VMEM((2, depth * cells // 2, owned), f32),
            dma((TAPS,)),
            dma((n, 2 * depth)),
            dma((n, 2 * depth)),
            dma((n, 2 * depth)),
            dma((n, 2 * depth)),
            dma((S, r, 2 * depth)),
            dma((nx, 2)),
            dma((nx, 2)),
            dma((nx, 2)),
            dma((nx, 2)),
        ],
        compiler_params=pltpu.CompilerParams(
            collective_id=0, has_side_effects=True, vmem_limit_bytes=62 * 1024 * 1024
        ),
    )(x, conv_weight)
    return jnp.transpose(result, (2, 0, 1))


def solution(mesh):
    return jax.shard_map(
        functools.partial(local, mesh.shape["space"], mesh.shape["chan"]),
        mesh=mesh,
        in_specs=(P("chan", ("groups", "space"), None), P(None, "chan", "space")),
        out_specs=P("chan", ("groups", "space"), None),
        check_vma=False,
    )
```

```python
import functools

import jax
import jax.numpy as jnp
from jax import lax
from jax.experimental import pallas as pl
from jax.experimental.pallas import tpu as pltpu
from jax.sharding import PartitionSpec as P

NZ = 16
TAPS = 27
MESH = pl.DeviceIdType.MESH


def kernel(
    S, n, r, x_ref, w_ref, out_ref,
    xz, xr, xs, wv, psend, precv, xsend, xrecv, own,
    w_sem, up_sem, down_sem, z_sem, a_send, a_recv, p_send, p_recv, q_send, q_recv,
):
    depth, cells, chb = x_ref.shape
    I = r * chb
    nx = S // 2
    planes = S * depth
    s = lax.axis_index("space")
    z = lax.axis_index("chan")
    x = s // 2
    k = s % 2
    partner = x * 2 + (1 - k)

    for t in range(TAPS):
        pltpu.make_async_copy(w_ref.at[t], wv.at[:, t * I : (t + 1) * I], w_sem.at[t]).start()

    barrier = pltpu.get_barrier_semaphore()

    for so in range(S):
        for step, there in ((-1, z > 0), (1, z < n - 1)):
            @pl.when(there)
            def _():
                pl.semaphore_signal(
                    barrier, inc=1, device_id={"space": lax.rem(s + so, S), "chan": z + step},
                    device_id_type=MESH,
                )

    for so in range(1, S):
        pl.semaphore_signal(
            barrier, inc=1, device_id={"space": lax.rem(s + so, S)}, device_id_type=MESH
        )
    here = jnp.where(z > 0, S, 0) + jnp.where(z < n - 1, S, 0) + (S - 1)
    pl.semaphore_wait(barrier, here)

    split = cells // 2 + NZ
    spans = ((0, split), (split, cells - split))
    rows_out = cells // 2

    def part(ref, u):
        return ref.at[u % depth, pl.ds(*spans[u // depth])]

    def hop(src, b, p, sem, to):
        return pltpu.make_async_remote_copy(
            src_ref=src, dst_ref=part(xz.at[b], p), send_sem=sem, recv_sem=z_sem.at[b, p],
            device_id={"chan": to}, device_id_type=MESH,
        )

    def across(src, b, p):
        return pltpu.make_async_remote_copy(
            src_ref=src, dst_ref=part(xr.at[s, b % r], p), send_sem=a_send.at[b, p],
            recv_sem=a_recv.at[s, b % r, p],
            device_id={"space": b // r}, device_id_type=MESH,
        )

    def source(h, b, p):
        return part(x_ref, p) if h == 0 else part(xz.at[b], p)

    def up(h, p):
        return hop(source(h, z - h, p), z - h, p, up_sem.at[h, p], z + 1)

    def down(h, p):
        return hop(source(h, z + h, p), z + h, p, down_sem.at[h, p], z - 1)

    def slanted(h, b, p, sem, to):
        return pltpu.make_async_remote_copy(
            src_ref=source(h, b, p), dst_ref=part(xr.at[s, b % r], p), send_sem=sem,
            recv_sem=a_recv.at[s, b % r, p],
            device_id={"space": b // r, "chan": to}, device_id_type=MESH,
        )

    def direct(h, b, to, end):
        return (to == end) & (b // r != s)

    def forward(h, p):
        for b, sign, end, send in ((z - h, 1, n - 1, up), (z + h, -1, 0, down)):
            valid = (b >= 0) & (b < n)
            relay = valid
            if h > 0:
                relay = valid & (z != end)

                @pl.when(relay)
                def _():
                    hop(part(xz.at[b], p), b, p, up_sem.at[0, p], z).wait_recv()

            if h < n - 1:
                straight = direct(h, b, z + sign, end)

                @pl.when(valid & (z != end) & ~straight)
                def _():
                    send(h, p).start()

                @pl.when(valid & (z != end) & straight)
                def _():
                    sem = (up_sem if sign == 1 else down_sem).at[h, p]
                    slanted(h, b, p, sem, z + sign).start()

            if h > 0 or sign == 1:
                @pl.when(relay & (b // r != s))
                def _():
                    across(source(h, b, p), b, p).start()

    for p in range(2 * depth):
        forward(0, p)

    zero_row = jnp.zeros((NZ, I), xs.dtype)
    zero_plane = jnp.zeros(xs.shape[2:], xs.dtype)
    for c in range(3):
        xs[0, c] = zero_plane
        xs[planes + 1, c] = zero_plane

        @pl.loop(1, planes + 1)
        def _(q):
            xs[q, c, :NZ, :] = zero_row
            xs[q, c, NZ + cells :, :] = zero_row

    def prepare(ref, u, q, j):
        v = part(ref, u)[...]
        start, size = spans[u // depth]
        rows = lax.broadcasted_iota(jnp.int32, (size, chb), 0) % NZ
        wide = v.astype(jnp.float32)
        before = jnp.where(rows == 0, 0.0, pltpu.roll(wide, 1, 0))
        after = jnp.where(rows == NZ - 1, 0.0, pltpu.roll(wide, size - 1, 0))
        lanes = slice(j * chb, (j + 1) * chb)
        to = slice(NZ + start, NZ + start + size)
        xs[q + 1, 0, to, lanes] = before.astype(xs.dtype)
        xs[q + 1, 1, to, lanes] = v
        xs[q + 1, 2, to, lanes] = after.astype(xs.dtype)

    for half in range(2):
        for h in range(1, n - 1):
            for p in range(depth):
                forward(h, half * depth + p)

    def fetch_half(half):
        for p in range(depth):
            u = half * depth + p
            for j in range(r):
                @pl.when(z == s * r + j)
                def _():
                    prepare(x_ref, u, s * depth + p, j)

                b = s * r + j

                @pl.when(((z == 0) & (b > 0)) | ((z == n - 1) & (b < n - 1)))
                def _():
                    hop(part(xz.at[b], u), b, u, up_sem.at[0, u], z).wait_recv()

                @pl.when(z != s * r + j)
                def _():
                    prepare(xz.at[s * r + j], u, s * depth + p, j)

            @pl.loop(1, S)
            def _(so):
                src = lax.rem(s + so, S)
                for j in range(r):
                    view = part(xr.at[src, j], u)
                    pltpu.make_async_remote_copy(
                        src_ref=view, dst_ref=view,
                        send_sem=a_send.at[0, u], recv_sem=a_recv.at[src, j, u],
                        device_id={"space": src}, device_id_type=MESH,
                    ).wait_recv()
                    prepare(xr.at[src, j], u, src * depth + p, j)

    for t in range(TAPS):
        pltpu.make_async_copy(w_ref.at[t], wv.at[:, t * I : (t + 1) * I], w_sem.at[t]).wait()

    def partial(dest, half):
        window = jnp.concatenate(
            [
                jnp.concatenate(
                    [
                        xs[
                            dest * depth + p + a, c,
                            NZ * b + half * rows_out : NZ * b + (half + 1) * rows_out, :,
                        ]
                        for p in range(depth)
                    ],
                    axis=0,
                )
                for a in range(3)
                for b in range(3)
                for c in range(3)
            ],
            axis=1,
        )
        return lax.dot_general(
            window, wv[...], (((1,), (1,)), ((), ())), preferred_element_type=jnp.float32
        )

    def target(hops, mine):
        far = lax.rem(x + hops, nx)
        return far * 2 + jnp.where(mine == 1, k, 1 - k)

    def half_of(ref, m, half):
        return ref.at[m, half]

    def to_partner(m, half):
        return pltpu.make_async_remote_copy(
            src_ref=half_of(psend, m, half), dst_ref=half_of(precv, m, half),
            send_sem=p_send.at[m, half], recv_sem=p_recv.at[m, half],
            device_id={"space": partner}, device_id_type=MESH,
        )

    def to_chip(m, half, there):
        return pltpu.make_async_remote_copy(
            src_ref=half_of(xsend, m, half), dst_ref=half_of(xrecv, m, half),
            send_sem=q_send.at[m, half], recv_sem=q_recv.at[m, half],
            device_id={"space": there}, device_id_type=MESH,
        )

    def reduce_half(half, first, stop):
        @pl.loop(2 * first, 2 * stop)
        def _(i):
            m = i // 2
            mine = i % 2
            total = partial(target(m + 1, mine), half)

            @pl.when(mine == 0)
            def _():
                psend[m, half] = total
                to_partner(m, half).start()

            @pl.when(mine == 1)
            def _():
                to_partner(m, half).wait_recv()
                if first < nx - 1:
                    xsend[m, half] = total + precv[m, half]
                    to_chip(m, half, target(m + 1, 1)).start()
                else:
                    own[half] = total + precv[m, half]

    fetch_half(0)
    reduce_half(0, 0, nx - 1)
    fetch_half(1)
    reduce_half(1, 0, nx - 1)
    for half in range(2):
        reduce_half(half, nx - 1, nx)

    for half in range(2):
        total = own[half]
        for m in range(nx - 1):
            to_chip(m, half, partner).wait_recv()
            total = total + xrecv[m, half]
        for p in range(depth):
            out_ref[p, half * rows_out : (half + 1) * rows_out, :] = total[
                p * rows_out : (p + 1) * rows_out
            ].astype(out_ref.dtype)

    for h in range(n):
        for p in range(2 * depth):
            if h < n - 1:
                @pl.when((z - h >= 0) & (z < n - 1))
                def _():
                    up(h, p).wait_send()

                @pl.when((z + h < n) & (z > 0))
                def _():
                    down(h, p).wait_send()

            for b, sign, end in ((z - h, 1, n - 1), (z + h, -1, 0)):
                relay = (b >= 0) & (b < n) & (b // r != s)
                if h > 0:
                    relay = relay & ~direct(h - 1, b, z, end)

                if h > 0 or sign == 1:
                    @pl.when(relay)
                    def _():
                        across(source(h, b, p), b, p).wait_send()

    for m in range(nx):
        for half in range(2):
            to_partner(m, half).wait_send()
            if m < nx - 1:
                to_chip(m, half, partner).wait_send()


def local(S, n, fields, conv_weight):
    chb, depth, cells = fields.shape
    owned, I = conv_weight.shape[1:]
    r = I // chb
    nx = S // 2
    planes = S * depth
    bf16, f32 = jnp.bfloat16, jnp.float32
    dma = pltpu.SemaphoreType.DMA
    x = jnp.transpose(fields, (1, 2, 0))
    result = pl.pallas_call(
        functools.partial(kernel, S, n, r),
        out_shape=jax.ShapeDtypeStruct((depth, cells, owned), bf16),
        in_specs=[
            pl.BlockSpec(memory_space=pltpu.VMEM),
            pl.BlockSpec(memory_space=pl.ANY),
        ],
        out_specs=pl.BlockSpec(memory_space=pltpu.VMEM),
        scratch_shapes=[
            pltpu.VMEM((n, depth, cells, chb), bf16),
            pltpu.VMEM((S, r, depth, cells, chb), bf16),
            pltpu.VMEM((planes + 2, 3, cells + 2 * NZ, I), bf16),
            pltpu.VMEM((owned, TAPS * I), bf16),
            pltpu.VMEM((nx, 2, depth * cells // 2, owned), f32),
            pltpu.VMEM((nx, 2, depth * cells // 2, owned), f32),
            pltpu.VMEM((nx - 1, 2, depth * cells // 2, owned), f32),
            pltpu.VMEM((nx - 1, 2, depth * cells // 2, owned), f32),
            pltpu.VMEM((2, depth * cells // 2, owned), f32),
            dma((TAPS,)),
            dma((n, 2 * depth)),
            dma((n, 2 * depth)),
            dma((n, 2 * depth)),
            dma((n, 2 * depth)),
            dma((S, r, 2 * depth)),
            dma((nx, 2)),
            dma((nx, 2)),
            dma((nx, 2)),
            dma((nx, 2)),
        ],
        compiler_params=pltpu.CompilerParams(
            collective_id=0, has_side_effects=True, vmem_limit_bytes=62 * 1024 * 1024
        ),
    )(x, conv_weight)
    return jnp.transpose(result, (2, 0, 1))


def solution(mesh):
    return jax.shard_map(
        functools.partial(local, mesh.shape["space"], mesh.shape["chan"]),
        mesh=mesh,
        in_specs=(P("chan", ("groups", "space"), None), P(None, "chan", "space")),
        out_specs=P("chan", ("groups", "space"), None),
        check_vma=False,
    )
```
